32 devices in a mesh: space: 16 (over z, x, core), mem: 2 (over y).
Axes of the slice: x: 2, y: 2, z: 4, core: 2. Of those that a mesh axis runs over, the one named last changes fastest.
Arguments:
- control: bfloat16 [16, 4096, 256], P('mem', 'space'), may hold values from -6 to 6
- perturbations: bfloat16 [16, 4096, 256], P('mem', 'space'), may hold values from -1.5 to 1.5
- innovation: float32 [4096, 256], P('space'), may hold values from -6 to 6
- error_weight: float32 [4096, 256], P('space'), may hold values from 0.3 to 3
Outputs:
- gradient: bfloat16 [16, 4096, 256], P('mem', 'space')
- increment: float32 [4096, 256], P('space', 'mem')
The draws below stay inside these ranges and needn't reach their ends.
All inputs are finite; a program needn't handle non-finite values.
Results may differ from the reference program's by a relative error of at most 0.0067.
Values may be sent and summed in bfloat16 or wider, within the bound.
A program may use at most 64 MiB of HBM per device.

```python
import math
import jax
import jax.numpy as jnp
from jax import lax

MEMBERS = 16
BAND = 256
ROWS_DEV = 256
ROWS = 4096
COLS = 256
ROW_SCALE = 192
COL_SCALE = 1


def block_levels(rng, extent, shards, least, largest):
    gain = 1.0
    for position, shards_of in shards:
        steps = jax.random.uniform(jax.random.fold_in(jax.random.fold_in(rng, 6), position), (shards_of,), jnp.float32, least / len(shards), largest / len(shards))
        gain = gain * jnp.repeat(jnp.exp(steps), extent[position] // shards_of).reshape((-1,) + (1,) * (len(extent) - 1 - position))
    return gain


def bell_draw(stream_key, dims, spread, bound, shards=(), held_as=jnp.bfloat16):
    gain = block_levels(stream_key, dims, shards, -0.22, 0.18) if shards else 1.0
    array = jax.random.normal(stream_key, dims, jnp.float32) * spread * gain
    return jnp.minimum(jnp.maximum(array, -bound), bound).astype(held_as)


def setup_inputs(seed: int = 0) -> dict:
    streams_of = jax.random.split(jax.random.key(seed), 5)
    control = bell_draw(streams_of[0], (MEMBERS, ROWS, COLS), 1.0, 6.0, ((0, 2), (1, 16)))
    perturbations = bell_draw(streams_of[1], (MEMBERS, ROWS, COLS), 0.25, 1.5, ((0, 2), (1, 16)))
    innovation = bell_draw(streams_of[2], (ROWS, COLS), 1.0, 6.0, ((0, 16),), jnp.float32)
    error_weight = jnp.clip(jnp.exp(math.log(3.0) - 2.3025851 * jax.random.uniform(streams_of[3], (ROWS, COLS), jnp.float32) ** block_levels(streams_of[3], (ROWS, COLS), ((0, 16),), -0.2, 0.2)), 0.3, 3.0)
    return dict(control=control, perturbations=perturbations, innovation=innovation, error_weight=error_weight)


def column_table(count):
    place = jnp.arange(count, dtype=jnp.float32)
    gap = place[:, None] - place[None, :]
    taper_factor = (COL_SCALE * math.sqrt(math.pi)) ** (-0.5)
    return (taper_factor * jnp.exp(-gap * gap / (2.0 * COL_SCALE * COL_SCALE))).astype(jnp.bfloat16)

def row_table(count):
    inner = jnp.arange(count, dtype=jnp.float32)[:, None]
    outer = jnp.arange(count + 2 * BAND, dtype=jnp.float32)[None, :]
    gap = inner + BAND - outer
    taper_factor = (ROW_SCALE * math.sqrt(math.pi)) ** (-0.5)
    values = taper_factor * jnp.exp(-gap * gap / (2.0 * ROW_SCALE * ROW_SCALE))
    return jnp.where(jnp.abs(gap) <= BAND, values, 0.0).astype(jnp.bfloat16)

def row_filter(depth_field, table):
    padded = jnp.pad(depth_field, ((BAND, BAND), (0, 0)))

    def single_block(block):
        window = lax.dynamic_slice_in_dim(padded, (block * ROWS_DEV).astype(jnp.int32), ROWS_DEV + 2 * BAND, 0)
        return jnp.dot(table, window, preferred_element_type=jnp.float32)
    blocks = lax.map(single_block, jnp.arange(ROWS // ROWS_DEV, dtype=jnp.int32))
    return blocks.reshape(ROWS, COLS)

def reference(control, perturbations, innovation, error_weight):
    column_lookup = column_table(COLS)
    rows_table = row_table(ROWS_DEV)

    def forward(total, pair):
        member_control, member_pert = pair
        smoothed = jnp.dot(member_control, column_lookup, preferred_element_type=jnp.float32).astype(jnp.bfloat16)
        localized = row_filter(smoothed, rows_table)
        return (total + member_pert.astype(jnp.float32) * localized, None)
    increment = lax.scan(forward, jnp.zeros((ROWS, COLS), jnp.float32), (control, perturbations))[0]
    weighted = lax.optimization_barrier((error_weight * (increment - innovation)).astype(jnp.bfloat16))

    def adjoint_sensitivity(member_pert):
        product = (member_pert.astype(jnp.float32) * weighted.astype(jnp.float32)).astype(jnp.bfloat16)
        product_columns = jnp.dot(product, column_lookup, preferred_element_type=jnp.float32).astype(jnp.bfloat16)
        return row_filter(product_columns, rows_table).astype(jnp.bfloat16)
    gradient = lax.map(adjoint_sensitivity, perturbations)
    return (gradient, increment)
```

```python
import functools
import math

import jax
import jax.numpy as jnp
from jax import lax
from jax.experimental import pallas as pl
from jax.experimental.pallas import tpu as pltpu
from jax.sharding import PartitionSpec as P

BAND = 256
ROW_SCALE = 192
COL_SCALE = 1
CHUNKS = 2
TILE = 16
MESH = pl.DeviceIdType.MESH


def taper(gap, scale):
    factor = (scale * math.sqrt(math.pi)) ** (-0.5)
    return factor * jnp.exp(-gap * gap / (2.0 * scale * scale))


def dot(a, b):
    return jnp.dot(a, b, preferred_element_type=jnp.float32)


def kernel(
    space_size, mem_size, share,
    control, pert, innovation, error_weight, gradient, increment,
    own_control, own_pert, own_innovation, own_weight,
    halo, local, centre, term_out, term_in, weighted, total, columns, result,
    col_table, row_table,
    load_sem, halo_send, halo_recv, term_send, term_recv,
    weight_send, weight_recv, inc_send, inc_recv, out_sem,
):
    members, rows, cols = control.shape
    step = rows // CHUNKS
    part = step // mem_size
    i = lax.axis_index("space")
    m = lax.axis_index("mem")
    has = {-1: i > 0, 1: i < space_size - 1}
    peers = [(db, dm) for db in (-1, 0, 1) for dm in range(mem_size) if (db, dm) != (0, 0)]

    def when(db, action):
        if db == 0:
            action()
        else:
            pl.when(has[db])(action)

    def device(db, dm):
        return {"space": i + db, "mem": lax.rem(m + dm + mem_size, mem_size)}

    def slot(db, dm):
        return (db + 1) * mem_size + dm

    def owned(chunk, owner):
        return pl.ds(pl.multiple_of(chunk * step + owner * part, part), part)

    def remote(src, dst, send, recv, target):
        return pltpu.make_async_remote_copy(
            src_ref=src, dst_ref=dst, send_sem=send, recv_sem=recv,
            device_id=target, device_id_type=MESH,
        )

    def halo_copy(db, chunk, target):
        side = 0 if db == 1 else 1
        span = pl.ds(chunk * step, step)
        return remote(
            pert.at[:, span, :], halo.at[side, :, span, :],
            halo_send.at[side, chunk], halo_recv.at[side, chunk], target,
        )

    def term_copy(db, dm, chunk, target):
        place = slot(db, dm)
        return remote(
            term_out.at[db + 1, owned(chunk, lax.rem(m + dm, mem_size)), :],
            term_in.at[chunk, place],
            term_send.at[chunk, place], term_recv.at[chunk, place], target,
        )

    def weight_copy(db, dm, chunk, owner, target):
        place = slot(db, dm)
        return remote(
            weighted.at[1, owned(chunk, owner), :], weighted.at[1 - db, owned(chunk, owner), :],
            weight_send.at[chunk, place], weight_recv.at[chunk, place], target,
        )

    def inc_copy(dm, chunk, owner, target):
        return remote(
            total.at[owned(chunk, owner), :], total.at[owned(chunk, owner), :],
            inc_send.at[chunk, dm], inc_recv.at[chunk, dm], target,
        )

    loads = [
        pltpu.make_async_copy(src, dst, load_sem.at[n])
        for n, (src, dst) in enumerate((
            (control, own_control), (pert, own_pert),
            (innovation, own_innovation), (error_weight, own_weight),
        ))
    ]
    for load in loads:
        load.start()

    barrier = pltpu.get_barrier_semaphore()
    for db, dm in peers:
        def greet(db=db, dm=dm):
            pl.semaphore_signal(barrier, inc=1, device_id=device(db, dm), device_id_type=MESH)
        when(db, greet)
    sides = has[-1].astype(jnp.int32) + has[1].astype(jnp.int32)
    pl.semaphore_wait(barrier, mem_size - 1 + mem_size * sides)

    for chunk in range(CHUNKS):
        for db in (1, -1):
            when(db, lambda db=db, chunk=chunk: halo_copy(db, chunk, device(db, 0)).start())

    for db in (-1, 1):
        def clear(db=db):
            side = 0 if db == -1 else 1
            halo[side] = jnp.zeros(halo.shape[1:], halo.dtype)
            weighted[1 + db] = jnp.zeros((rows, cols), weighted.dtype)
            for dm in range(mem_size):
                for chunk in range(CHUNKS):
                    term_in[chunk, slot(-db, dm)] = jnp.zeros((part, cols), term_in.dtype)
        pl.when(jnp.logical_not(has[db]))(clear)

    inner = lax.broadcasted_iota(jnp.int32, (rows, rows), 0).astype(jnp.float32)
    outer = lax.broadcasted_iota(jnp.int32, (rows, rows), 1).astype(jnp.float32)
    for block in range(3):
        gap = inner - outer + BAND * (1 - block)
        values = jnp.where(jnp.abs(gap) <= BAND, taper(gap, ROW_SCALE), 0.0)
        row_table[:, block * rows:(block + 1) * rows] = values.astype(jnp.bfloat16)
    place = lax.broadcasted_iota(jnp.int32, (cols, cols), 0).astype(jnp.float32)
    other = lax.broadcasted_iota(jnp.int32, (cols, cols), 1).astype(jnp.float32)
    col_table[...] = taper(place - other, COL_SCALE).astype(jnp.bfloat16)
    centre[...] = jnp.zeros_like(centre)

    for load in loads:
        load.wait()

    def forward(k, carry):
        smoothed = dot(own_control[k], col_table[...]).astype(jnp.bfloat16)
        local[0, k] = dot(row_table[:, 2 * rows:], smoothed)
        local[1, k] = dot(row_table[:, :rows], smoothed)
        centre[...] += own_pert[k].astype(jnp.float32) * dot(row_table[:, rows:2 * rows], smoothed)
        return carry

    lax.fori_loop(0, members, forward, 0)
    term_out[1] = centre[...].astype(jnp.bfloat16)
    for chunk in range(CHUNKS):
        for dm in range(1, mem_size):
            term_copy(0, dm, chunk, device(0, dm)).start()

    def send_terms(chunk):
        for db in (-1, 1):
            def terms(db=db):
                side = 0 if db == -1 else 1
                halo_copy(-db, chunk, device(db, 0)).wait_recv()

                def tile(t, carry):
                    span = pl.ds(pl.multiple_of(chunk * step + t * TILE, TILE), TILE)
                    acc = jnp.zeros((TILE, cols), jnp.float32)
                    for k in range(members):
                        acc += halo[side, k, span, :].astype(jnp.float32) * local[side, k, span, :]
                    term_out[db + 1, span, :] = acc.astype(jnp.bfloat16)
                    return carry

                lax.fori_loop(0, step // TILE, tile, 0)
                for dm in range(mem_size):
                    term_copy(db, dm, chunk, device(db, dm)).start()
            when(db, terms)

    def send_weighted(chunk):
        for db, dm in peers:
            when(-db, lambda db=db, dm=dm: term_copy(db, dm, chunk, device(-db, -dm)).wait_recv())
        span = owned(chunk, m)
        sums = centre[span, :]
        for db, dm in peers:
            sums += term_in[chunk, slot(db, dm)].astype(jnp.float32)
        total[span, :] = sums
        weighted[1, span, :] = (
            own_weight[span, :] * (sums - own_innovation[span, :])
        ).astype(jnp.bfloat16)
        for db, dm in peers:
            when(db, lambda db=db, dm=dm: weight_copy(db, dm, chunk, m, device(db, dm)).start())
        for dm in range(1, mem_size):
            inc_copy(dm, chunk, m, device(0, dm)).start()

    def adjoint_cols(chunk):
        for db, dm in peers:
            owner = lax.rem(m - dm + mem_size, mem_size)
            when(-db, lambda db=db, dm=dm, owner=owner: weight_copy(
                db, dm, chunk, owner, device(-db, -dm)).wait_recv())
        span = pl.ds(chunk * step, step)

        def member(k, carry):
            fields = (halo[0, k, span, :], own_pert[k, span, :], halo[1, k, span, :])
            for block, field in enumerate(fields):
                product = field * weighted[block, span, :]
                columns[k, pl.ds(block * rows + chunk * step, step), :] = dot(
                    product, col_table[...]
                ).astype(jnp.bfloat16)
            return carry

        lax.fori_loop(0, members, member, 0)

    for turn in range(CHUNKS + 2):
        if turn < CHUNKS:
            send_terms(turn)
        if 0 <= turn - 1 < CHUNKS:
            send_weighted(turn - 1)
        if 0 <= turn - 2 < CHUNKS:
            adjoint_cols(turn - 2)

    def out_copy(k):
        return pltpu.make_async_copy(result.at[k], gradient.at[k], out_sem.at[k])

    def last(k, carry):
        result[k] = dot(row_table[...], columns[k]).astype(jnp.bfloat16)
        out_copy(k).start()
        return carry

    lax.fori_loop(0, members, last, 0)

    for chunk in range(CHUNKS):
        for dm in range(1, mem_size):
            owner = lax.rem(m - dm + mem_size, mem_size)
            inc_copy(dm, chunk, owner, device(0, -dm)).wait_recv()
    if increment.shape[1] == cols:
        view = total
    else:
        view = total.at[:, pl.ds(pl.multiple_of(m * share, share), share)]
    inc_out = pltpu.make_async_copy(view, increment, load_sem.at[0])
    inc_out.start()

    for chunk in range(CHUNKS):
        for db in (1, -1):
            when(db, lambda db=db, chunk=chunk: halo_copy(db, chunk, device(db, 0)).wait_send())
        for db, dm in peers:
            def sent(db=db, dm=dm, chunk=chunk):
                term_copy(db, dm, chunk, device(db, dm)).wait_send()
                weight_copy(db, dm, chunk, m, device(db, dm)).wait_send()
            when(db, sent)
        for dm in range(1, mem_size):
            inc_copy(dm, chunk, m, device(0, dm)).wait_send()
    for k in range(members):
        out_copy(k).wait()
    inc_out.wait()


def on_device(control, perturbations, innovation, error_weight):
    members, rows, cols = control.shape
    space_size = lax.axis_size("space")
    mem_size = lax.axis_size("mem")
    share = cols // mem_size
    aligned = share % 128 == 0
    part = rows // CHUNKS // mem_size
    slots = 3 * mem_size
    bf16, f32 = jnp.bfloat16, jnp.float32
    dma = pltpu.SemaphoreType.DMA
    gradient, increment = pl.pallas_call(
        functools.partial(kernel, space_size, mem_size, share),
        out_shape=(
            jax.ShapeDtypeStruct((members, rows, cols), bf16),
            jax.ShapeDtypeStruct((rows, share if aligned else cols), f32),
        ),
        in_specs=[pl.BlockSpec(memory_space=pl.ANY)] * 4,
        out_specs=(pl.BlockSpec(memory_space=pl.ANY),) * 2,
        scratch_shapes=[
            pltpu.VMEM((members, rows, cols), bf16),
            pltpu.VMEM((members, rows, cols), bf16),
            pltpu.VMEM((rows, cols), f32),
            pltpu.VMEM((rows, cols), f32),
            pltpu.VMEM((2, members, rows, cols), bf16),
            pltpu.VMEM((2, members, rows, cols), f32),
            pltpu.VMEM((rows, cols), f32),
            pltpu.VMEM((3, rows, cols), bf16),
            pltpu.VMEM((CHUNKS, slots, part, cols), bf16),
            pltpu.VMEM((3, rows, cols), bf16),
            pltpu.VMEM((rows, cols), f32),
            pltpu.VMEM((members, 3 * rows, cols), bf16),
            pltpu.VMEM((members, rows, cols), bf16),
            pltpu.VMEM((cols, cols), bf16),
            pltpu.VMEM((rows, 3 * rows), bf16),
            dma((4,)),
            dma((2, CHUNKS)),
            dma((2, CHUNKS)),
            dma((CHUNKS, slots)),
            dma((CHUNKS, slots)),
            dma((CHUNKS, slots)),
            dma((CHUNKS, slots)),
            dma((CHUNKS, mem_size)),
            dma((CHUNKS, mem_size)),
            dma((members,)),
        ],
        compiler_params=pltpu.CompilerParams(
            collective_id=0, has_side_effects=True, vmem_limit_bytes=40 * 1024 * 1024
        ),
    )(control, perturbations, innovation, error_weight)
    if not aligned:
        increment = lax.dynamic_slice_in_dim(increment, lax.axis_index("mem") * share, share, 1)
    return gradient, increment


def solution(mesh):
    placed = (P("mem", "space", None), P("mem", "space", None), P("space", None), P("space", None))
    return jax.shard_map(
        on_device,
        mesh=mesh,
        in_specs=placed,
        out_specs=(P("mem", "space", None), P("space", "mem")),
        check_vma=False,
    )
```

```python
import functools
import math

import jax
import jax.numpy as jnp
from jax import lax
from jax.experimental import pallas as pl
from jax.experimental.pallas import tpu as pltpu
from jax.sharding import PartitionSpec as P

BAND = 256
ROW_SCALE = 192
COL_SCALE = 1
SIZES = (4, 4)
CHUNKS = len(SIZES)
TILE = 16
UNROLL = 4
MESH = pl.DeviceIdType.MESH


def taper(gap, scale):
    factor = (scale * math.sqrt(math.pi)) ** (-0.5)
    return factor * jnp.exp(-gap * gap / (2.0 * scale * scale))


def dot(a, b):
    return jnp.dot(a, b, preferred_element_type=jnp.float32)


def kernel(
    space_size, mem_size, share,
    control, pert, innovation, error_weight, gradient, increment,
    own_control, own_pert, own_innovation, own_weight,
    halo, local, centre, term_out, term_in, weighted, total, result,
    col_table, row_table, *rest,
):
    tables, adjoints = rest[:CHUNKS], rest[CHUNKS:2 * CHUNKS]
    (accumulated, load_sem, halo_send, halo_recv, term_send, term_recv,
    weight_send, weight_recv, inc_send, inc_recv, out_sem) = rest[2 * CHUNKS:]
    members, rows, cols = control.shape
    steps = [rows * size // 8 for size in SIZES]
    starts = [sum(steps[:n]) for n in range(CHUNKS)]
    i = lax.axis_index("space")
    m = lax.axis_index("mem")
    has = {-1: i > 0, 1: i < space_size - 1}
    peers = [(db, dm) for db in (-1, 0, 1) for dm in range(mem_size) if (db, dm) != (0, 0)]

    def when(db, action):
        if db == 0:
            action()
        else:
            pl.when(has[db])(action)

    def device(db, dm):
        return {"space": i + db, "mem": lax.rem(m + dm + mem_size, mem_size)}

    def slot(db, dm):
        return (db + 1) * mem_size + dm

    aligned = share % 128 == 0
    inc_peers = [] if aligned else list(range(1, mem_size))

    def owned(chunk, owner):
        if aligned:
            return rows_of(chunk), pl.ds(pl.multiple_of(owner * share, share), share)
        part = steps[chunk] // mem_size
        first = starts[chunk] + owner * part
        return pl.ds(pl.multiple_of(first, math.gcd(starts[chunk], part)), part), slice(None)

    def rows_of(chunk):
        return pl.ds(starts[chunk], steps[chunk])

    def terms_of(chunk, place):
        if aligned:
            return place, rows_of(chunk), slice(None)
        return place, pl.ds(starts[chunk] // mem_size, steps[chunk] // mem_size), slice(None)

    def remote(src, dst, send, recv, target):
        return pltpu.make_async_remote_copy(
            src_ref=src, dst_ref=dst, send_sem=send, recv_sem=recv,
            device_id=target, device_id_type=MESH,
        )

    def halo_copy(db, chunk, target):
        side = 0 if db == 1 else 1
        span = rows_of(chunk)
        return remote(
            pert.at[:, span, :], halo.at[side, :, span, :],
            halo_send.at[side, chunk], halo_recv.at[side, chunk], target,
        )

    def term_copy(db, dm, chunk, target):
        place = slot(db, dm)
        return remote(
            term_out.at[db + 1, *owned(chunk, lax.rem(m + dm, mem_size))],
            term_in.at[terms_of(chunk, place)],
            term_send.at[chunk, place], term_recv.at[chunk, place], target,
        )

    def weight_copy(db, dm, chunk, owner, target):
        place = slot(db, dm)
        return remote(
            weighted.at[1, *owned(chunk, owner)], weighted.at[1 - db, *owned(chunk, owner)],
            weight_send.at[chunk, place], weight_recv.at[chunk, place], target,
        )

    def inc_copy(dm, chunk, owner, target):
        return remote(
            total.at[owned(chunk, owner)], total.at[owned(chunk, owner)],
            inc_send.at[chunk, dm], inc_recv.at[chunk, dm], target,
        )

    loads = [
        pltpu.make_async_copy(src, dst, load_sem.at[n])
        for n, (src, dst) in enumerate((
            (control, own_control), (pert, own_pert),
            (innovation, own_innovation), (error_weight, own_weight),
        ))
    ]
    for load in loads:
        load.start()

    barrier = pltpu.get_barrier_semaphore()
    for db, dm in peers:
        def greet(db=db, dm=dm):
            pl.semaphore_signal(barrier, inc=1, device_id=device(db, dm), device_id_type=MESH)
        when(db, greet)
    sides = has[-1].astype(jnp.int32) + has[1].astype(jnp.int32)
    pl.semaphore_wait(barrier, mem_size - 1 + mem_size * sides)

    for chunk in range(CHUNKS):
        for db in (1, -1):
            when(db, lambda db=db, chunk=chunk: halo_copy(db, chunk, device(db, 0)).start())

    for db in (-1, 1):
        def clear(db=db):
            side = 0 if db == -1 else 1
            halo[side] = jnp.zeros(halo.shape[1:], halo.dtype)
            weighted[1 + db] = jnp.zeros((rows, cols), weighted.dtype)
            for dm in range(mem_size):
                term_in[slot(-db, dm)] = jnp.zeros(term_in.shape[1:], term_in.dtype)
        pl.when(jnp.logical_not(has[db]))(clear)

    inner = lax.broadcasted_iota(jnp.int32, (rows, rows), 0).astype(jnp.float32)
    outer = lax.broadcasted_iota(jnp.int32, (rows, rows), 1).astype(jnp.float32)
    for block in range(3):
        gap = inner - outer + BAND * (1 - block)
        values = jnp.where(jnp.abs(gap) <= BAND, taper(gap, ROW_SCALE), 0.0)
        row_table[:, block * rows:(block + 1) * rows] = values.astype(jnp.bfloat16)
    for chunk in range(CHUNKS):
        size = steps[chunk]
        inner = lax.broadcasted_iota(jnp.int32, (rows, 3 * size), 0).astype(jnp.float32)
        outer = lax.broadcasted_iota(jnp.int32, (rows, 3 * size), 1)
        block = (outer >= size).astype(jnp.int32) + (outer >= 2 * size).astype(jnp.int32)
        gap = inner - (outer + starts[chunk] - BAND + block * (rows - size)).astype(jnp.float32)
        values = jnp.where(jnp.abs(gap) <= BAND, taper(gap, ROW_SCALE), 0.0)
        tables[chunk][...] = values.astype(jnp.bfloat16)
    place = lax.broadcasted_iota(jnp.int32, (cols, cols), 0).astype(jnp.float32)
    other = lax.broadcasted_iota(jnp.int32, (cols, cols), 1).astype(jnp.float32)
    col_table[...] = taper(place - other, COL_SCALE).astype(jnp.bfloat16)
    centre[...] = jnp.zeros_like(centre)

    for load in loads:
        load.wait()

    def forward(k, carry):
        smoothed = dot(own_control[k], col_table[...]).astype(jnp.bfloat16)
        local[0, k] = dot(row_table[:, 2 * rows:], smoothed)
        local[1, k] = dot(row_table[:, :rows], smoothed)
        centre[...] += own_pert[k].astype(jnp.float32) * dot(row_table[:, rows:2 * rows], smoothed)
        return carry

    lax.fori_loop(0, members, forward, 0)
    term_out[1] = centre[...].astype(jnp.bfloat16)
    for chunk in range(CHUNKS):
        for dm in range(1, mem_size):
            term_copy(0, dm, chunk, device(0, dm)).start()

    def send_terms(chunk, db, side):
        def terms():
            span = rows_of(chunk)
            remote(
                pert.at[:, span, :], halo.at[side, :, span, :],
                halo_send.at[side, chunk], halo_recv.at[side, chunk], device(db, 0),
            ).wait_recv()

            def tile(t, carry):
                span = pl.ds(pl.multiple_of(starts[chunk] + t * TILE, TILE), TILE)
                acc = jnp.zeros((TILE, cols), jnp.float32)
                for k in range(members):
                    acc += halo[side, k, span, :].astype(jnp.float32) * local[side, k, span, :]
                term_out[db + 1, span, :] = acc.astype(jnp.bfloat16)
                return carry

            lax.fori_loop(0, steps[chunk] // TILE, tile, 0)
            for dm in range(mem_size):
                term_copy(db, dm, chunk, device(db, dm)).start()
        pl.when(jnp.logical_and(i + db >= 0, i + db < space_size))(terms)

    odd = lax.rem(i, 2)
    for chunk in range(CHUNKS):
        send_terms(chunk, 1 - 2 * odd, 1 - odd)

    def send_weighted(chunk):
        for db, dm in peers:
            when(-db, lambda db=db, dm=dm: term_copy(db, dm, chunk, device(-db, -dm)).wait_recv())
        span = owned(chunk, m)
        sums = centre[span]
        for db, dm in peers:
            sums += term_in[terms_of(chunk, slot(db, dm))].astype(jnp.float32)
        total[span] = sums
        weighted[1, *span] = (
            own_weight[span] * (sums - own_innovation[span])
        ).astype(jnp.bfloat16)
        for db, dm in peers:
            when(db, lambda db=db, dm=dm: weight_copy(db, dm, chunk, m, device(db, dm)).start())
        for dm in inc_peers:
            inc_copy(dm, chunk, m, device(0, dm)).start()

    def adjoint_cols(chunk):
        for db, dm in peers:
            owner = lax.rem(m - dm + mem_size, mem_size)
            when(-db, lambda db=db, dm=dm, owner=owner: weight_copy(
                db, dm, chunk, owner, device(-db, -dm)).wait_recv())
        span = rows_of(chunk)

        final = chunk == CHUNKS - 1

        def member(k, carry):
            fields = (halo[0, k, span, :], own_pert[k, span, :], halo[1, k, span, :])
            for block, field in enumerate(fields):
                product = field * weighted[block, span, :]
                adjoints[chunk][k, block * steps[chunk]:(block + 1) * steps[chunk], :] = dot(
                    product, col_table[...]
                ).astype(jnp.bfloat16)
            sums = dot(tables[chunk][...], adjoints[chunk][k])
            if chunk:
                sums += accumulated[k]
            if final:
                result[k] = sums.astype(jnp.bfloat16)
                out_copy(k).start()
            else:
                accumulated[k] = sums
            return carry

        lax.fori_loop(0, members, member, 0, unroll=UNROLL)

    def out_copy(k):
        return pltpu.make_async_copy(result.at[k], gradient.at[k], out_sem.at[k])

    for turn in range(CHUNKS + 2):
        if turn < CHUNKS:
            send_terms(turn, 2 * odd - 1, odd)
        if 0 <= turn - 1 < CHUNKS:
            send_weighted(turn - 1)
        if 0 <= turn - 2 < CHUNKS:
            adjoint_cols(turn - 2)

    for chunk in range(CHUNKS):
        for dm in inc_peers:
            owner = lax.rem(m - dm + mem_size, mem_size)
            inc_copy(dm, chunk, owner, device(0, -dm)).wait_recv()
    if increment.shape[1] == cols:
        view = total
    else:
        view = total.at[:, pl.ds(pl.multiple_of(m * share, share), share)]
    inc_out = pltpu.make_async_copy(view, increment, load_sem.at[0])
    inc_out.start()

    for chunk in range(CHUNKS):
        for db in (1, -1):
            when(db, lambda db=db, chunk=chunk: halo_copy(db, chunk, device(db, 0)).wait_send())
        for db, dm in peers:
            def sent(db=db, dm=dm, chunk=chunk):
                term_copy(db, dm, chunk, device(db, dm)).wait_send()
                weight_copy(db, dm, chunk, m, device(db, dm)).wait_send()
            when(db, sent)
        for dm in inc_peers:
            inc_copy(dm, chunk, m, device(0, dm)).wait_send()
    for k in range(members):
        out_copy(k).wait()
    inc_out.wait()


def deliver(gradient, increment, gradient_out, increment_out, held, held_increment, in_sem, out_sem):
    members = gradient.shape[0]
    steps = [(gradient.at[k], held.at[k], gradient_out.at[k]) for k in range(members)]
    steps.append((increment, held_increment, increment_out))
    arrivals = [pltpu.make_async_copy(src, mid, in_sem.at[n]) for n, (src, mid, _) in enumerate(steps)]
    leaves = [pltpu.make_async_copy(mid, dst, out_sem.at[n]) for n, (_, mid, dst) in enumerate(steps)]
    for copy in arrivals:
        copy.start()
    for arrival, leave in zip(arrivals, leaves):
        arrival.wait()
        leave.start()
    for leave in leaves:
        leave.wait()


def on_device(control, perturbations, innovation, error_weight):
    members, rows, cols = control.shape
    space_size = lax.axis_size("space")
    mem_size = lax.axis_size("mem")
    share = cols // mem_size
    aligned = share % 128 == 0
    steps = [rows * size // 8 for size in SIZES]
    slots = 3 * mem_size
    bf16, f32 = jnp.bfloat16, jnp.float32
    dma = pltpu.SemaphoreType.DMA
    gradient, increment = pl.pallas_call(
        functools.partial(kernel, space_size, mem_size, share),
        out_shape=(
            jax.ShapeDtypeStruct((members, rows, cols), bf16),
            jax.ShapeDtypeStruct((rows, share if aligned else cols), f32),
        ),
        in_specs=[pl.BlockSpec(memory_space=pltpu.HBM)] * 4,
        out_specs=(pl.BlockSpec(memory_space=pl.ANY),) * 2,
        scratch_shapes=[
            pltpu.VMEM((members, rows, cols), bf16),
            pltpu.VMEM((members, rows, cols), bf16),
            pltpu.VMEM((rows, cols), f32),
            pltpu.VMEM((rows, cols), f32),
            pltpu.VMEM((2, members, rows, cols), bf16),
            pltpu.VMEM((2, members, rows, cols), f32),
            pltpu.VMEM((rows, cols), f32),
            pltpu.VMEM((3, rows, cols), bf16),
            pltpu.VMEM((slots, rows, share) if aligned else (slots, rows // mem_size, cols), bf16),
            pltpu.VMEM((3, rows, cols), bf16),
            pltpu.VMEM((rows, cols), f32),
            pltpu.VMEM((members, rows, cols), bf16),
            pltpu.VMEM((cols, cols), bf16),
            pltpu.VMEM((rows, 3 * rows), bf16),
            *[pltpu.VMEM((rows, 3 * step), bf16) for step in steps],
            *[pltpu.VMEM((members, 3 * step, cols), bf16) for step in steps],
            pltpu.VMEM((members, rows, cols), f32),
            dma((4,)),
            dma((2, CHUNKS)),
            dma((2, CHUNKS)),
            dma((CHUNKS, slots)),
            dma((CHUNKS, slots)),
            dma((CHUNKS, slots)),
            dma((CHUNKS, slots)),
            dma((CHUNKS, mem_size)),
            dma((CHUNKS, mem_size)),
            dma((members,)),
        ],
        compiler_params=pltpu.CompilerParams(
            collective_id=0, has_side_effects=True, vmem_limit_bytes=60 * 1024 * 1024
        ),
    )(control, perturbations, innovation, error_weight)
    if not aligned:
        increment = lax.dynamic_slice_in_dim(increment, lax.axis_index("mem") * share, share, 1)
    return pl.pallas_call(
        deliver,
        out_shape=(
            jax.ShapeDtypeStruct((members, rows, cols), bf16),
            jax.ShapeDtypeStruct((rows, share), f32),
        ),
        in_specs=[pl.BlockSpec(memory_space=pl.ANY)] * 2,
        out_specs=(pl.BlockSpec(memory_space=pl.ANY),) * 2,
        scratch_shapes=[
            pltpu.VMEM((members, rows, cols), bf16),
            pltpu.VMEM((rows, share), f32),
            dma((members + 1,)),
            dma((members + 1,)),
        ],
    )(gradient, increment)


def solution(mesh):
    placed = (P("mem", "space", None), P("mem", "space", None), P("space", None), P("space", None))
    return jax.shard_map(
        on_device,
        mesh=mesh,
        in_specs=placed,
        out_specs=(P("mem", "space", None), P("space", "mem")),
        check_vma=False,
    )
```

```python
import functools
import math

import jax
import jax.numpy as jnp
from jax import lax
from jax.experimental import pallas as pl
from jax.experimental.pallas import tpu as pltpu
from jax.sharding import PartitionSpec as P

BAND = 256
ROW_SCALE = 192
COL_SCALE = 1
SIZES = (4, 4)
CHUNKS = len(SIZES)
TILE = 16
UNROLL = 8
MESH = pl.DeviceIdType.MESH


def taper(gap, scale):
    factor = (scale * math.sqrt(math.pi)) ** (-0.5)
    return factor * jnp.exp(-gap * gap / (2.0 * scale * scale))


def dot(a, b):
    return jnp.dot(a, b, preferred_element_type=jnp.float32)


def kernel(
    space_size, mem_size, share,
    control, pert, innovation, error_weight, gradient, increment,
    own_control, own_pert, own_innovation, own_weight,
    halo, local, centre, term_out, term_in, weighted, total, result,
    col_table, row_table, *rest,
):
    tables, adjoints = rest[:CHUNKS], rest[CHUNKS:2 * CHUNKS]
    (accumulated, load_sem, halo_send, halo_recv, term_send, term_recv,
    weight_send, weight_recv, inc_send, inc_recv, out_sem) = rest[2 * CHUNKS:]
    members, rows, cols = control.shape
    steps = [rows * size // 8 for size in SIZES]
    starts = [sum(steps[:n]) for n in range(CHUNKS)]
    i = lax.axis_index("space")
    m = lax.axis_index("mem")
    has = {-1: i > 0, 1: i < space_size - 1}
    peers = [(db, dm) for db in (-1, 0, 1) for dm in range(mem_size) if (db, dm) != (0, 0)]

    def when(db, action):
        if db == 0:
            action()
        else:
            pl.when(has[db])(action)

    def device(db, dm):
        return {"space": i + db, "mem": lax.rem(m + dm + mem_size, mem_size)}

    def slot(db, dm):
        return (db + 1) * mem_size + dm

    aligned = share % 128 == 0
    inc_peers = [] if aligned else list(range(1, mem_size))

    def owned(chunk, owner):
        if aligned:
            return rows_of(chunk), pl.ds(pl.multiple_of(owner * share, share), share)
        part = steps[chunk] // mem_size
        first = starts[chunk] + owner * part
        return pl.ds(pl.multiple_of(first, math.gcd(starts[chunk], part)), part), slice(None)

    def rows_of(chunk):
        return pl.ds(starts[chunk], steps[chunk])

    def terms_of(chunk, place):
        if aligned:
            return place, rows_of(chunk), slice(None)
        return place, pl.ds(starts[chunk] // mem_size, steps[chunk] // mem_size), slice(None)

    def remote(src, dst, send, recv, target):
        return pltpu.make_async_remote_copy(
            src_ref=src, dst_ref=dst, send_sem=send, recv_sem=recv,
            device_id=target, device_id_type=MESH,
        )

    def halo_copy(db, chunk, target):
        side = 0 if db == 1 else 1
        span = rows_of(chunk)
        return remote(
            pert.at[:, span, :], halo.at[side, :, span, :],
            halo_send.at[side, chunk], halo_recv.at[side, chunk], target,
        )

    def term_copy(db, dm, chunk, target):
        place = slot(db, dm)
        return remote(
            term_out.at[db + 1, *owned(chunk, lax.rem(m + dm, mem_size))],
            term_in.at[terms_of(chunk, place)],
            term_send.at[chunk, place], term_recv.at[chunk, place], target,
        )

    def weight_copy(db, dm, chunk, owner, target):
        place = slot(db, dm)
        return remote(
            weighted.at[1, *owned(chunk, owner)], weighted.at[1 - db, *owned(chunk, owner)],
            weight_send.at[chunk, place], weight_recv.at[chunk, place], target,
        )

    def inc_copy(dm, chunk, owner, target):
        return remote(
            total.at[owned(chunk, owner)], total.at[owned(chunk, owner)],
            inc_send.at[chunk, dm], inc_recv.at[chunk, dm], target,
        )

    loads = [
        pltpu.make_async_copy(src, dst, load_sem.at[n])
        for n, (src, dst) in enumerate((
            (control, own_control), (pert, own_pert),
            (innovation, own_innovation), (error_weight, own_weight),
        ))
    ]
    for load in loads:
        load.start()

    barrier = pltpu.get_barrier_semaphore()
    for db, dm in peers:
        def greet(db=db, dm=dm):
            pl.semaphore_signal(barrier, inc=1, device_id=device(db, dm), device_id_type=MESH)
        when(db, greet)
    sides = has[-1].astype(jnp.int32) + has[1].astype(jnp.int32)
    pl.semaphore_wait(barrier, mem_size - 1 + mem_size * sides)

    odd = lax.rem(i, 2)
    for db, side in ((2 * odd - 1, 1 - odd), (1 - 2 * odd, odd)):
        for chunk in range(CHUNKS):
            def send(db=db, side=side, chunk=chunk):
                span = rows_of(chunk)
                remote(
                    pert.at[:, span, :], halo.at[side, :, span, :],
                    halo_send.at[side, chunk], halo_recv.at[side, chunk], device(db, 0),
                ).start()
            pl.when(jnp.logical_and(i + db >= 0, i + db < space_size))(send)

    for db in (-1, 1):
        def clear(db=db):
            side = 0 if db == -1 else 1
            halo[side] = jnp.zeros(halo.shape[1:], halo.dtype)
            weighted[1 + db] = jnp.zeros((rows, cols), weighted.dtype)
            for dm in range(mem_size):
                term_in[slot(-db, dm)] = jnp.zeros(term_in.shape[1:], term_in.dtype)
        pl.when(jnp.logical_not(has[db]))(clear)

    inner = lax.broadcasted_iota(jnp.int32, (rows, rows), 0).astype(jnp.float32)
    outer = lax.broadcasted_iota(jnp.int32, (rows, rows), 1).astype(jnp.float32)
    for block in range(3):
        gap = inner - outer + BAND * (1 - block)
        values = jnp.where(jnp.abs(gap) <= BAND, taper(gap, ROW_SCALE), 0.0)
        row_table[:, block * rows:(block + 1) * rows] = values.astype(jnp.bfloat16)
    for chunk in range(CHUNKS):
        size = steps[chunk]
        inner = lax.broadcasted_iota(jnp.int32, (rows, 3 * size), 0).astype(jnp.float32)
        outer = lax.broadcasted_iota(jnp.int32, (rows, 3 * size), 1)
        block = (outer >= size).astype(jnp.int32) + (outer >= 2 * size).astype(jnp.int32)
        gap = inner - (outer + starts[chunk] - BAND + block * (rows - size)).astype(jnp.float32)
        values = jnp.where(jnp.abs(gap) <= BAND, taper(gap, ROW_SCALE), 0.0)
        tables[chunk][...] = values.astype(jnp.bfloat16)
    place = lax.broadcasted_iota(jnp.int32, (cols, cols), 0).astype(jnp.float32)
    other = lax.broadcasted_iota(jnp.int32, (cols, cols), 1).astype(jnp.float32)
    col_table[...] = taper(place - other, COL_SCALE).astype(jnp.bfloat16)
    centre[...] = jnp.zeros_like(centre)

    for load in loads:
        load.wait()

    def forward(k, carry):
        smoothed = dot(own_control[k], col_table[...]).astype(jnp.bfloat16)
        local[0, k] = dot(row_table[:, 2 * rows:], smoothed)
        local[1, k] = dot(row_table[:, :rows], smoothed)
        centre[...] += own_pert[k].astype(jnp.float32) * dot(row_table[:, rows:2 * rows], smoothed)
        return carry

    lax.fori_loop(0, members, forward, 0)
    term_out[1] = centre[...].astype(jnp.bfloat16)
    for chunk in range(CHUNKS):
        for dm in range(1, mem_size):
            term_copy(0, dm, chunk, device(0, dm)).start()

    def send_terms(chunk, db, side):
        def terms():
            span = rows_of(chunk)
            remote(
                pert.at[:, span, :], halo.at[side, :, span, :],
                halo_send.at[side, chunk], halo_recv.at[side, chunk], device(db, 0),
            ).wait_recv()

            def tile(t, carry):
                span = pl.ds(pl.multiple_of(starts[chunk] + t * TILE, TILE), TILE)
                acc = jnp.zeros((TILE, cols), jnp.float32)
                for k in range(members):
                    acc += halo[side, k, span, :].astype(jnp.float32) * local[side, k, span, :]
                term_out[db + 1, span, :] = acc.astype(jnp.bfloat16)
                return carry

            lax.fori_loop(0, steps[chunk] // TILE, tile, 0)
            for dm in range(mem_size):
                term_copy(db, dm, chunk, device(db, dm)).start()
        pl.when(jnp.logical_and(i + db >= 0, i + db < space_size))(terms)

    for chunk in range(CHUNKS):
        send_terms(chunk, 1 - 2 * odd, 1 - odd)

    def send_weighted(chunk):
        for db, dm in peers:
            when(-db, lambda db=db, dm=dm: term_copy(db, dm, chunk, device(-db, -dm)).wait_recv())
        span = owned(chunk, m)
        sums = centre[span]
        for db, dm in peers:
            sums += term_in[terms_of(chunk, slot(db, dm))].astype(jnp.float32)
        total[span] = sums
        weighted[1, *span] = (
            own_weight[span] * (sums - own_innovation[span])
        ).astype(jnp.bfloat16)
        for db, dm in peers:
            when(db, lambda db=db, dm=dm: weight_copy(db, dm, chunk, m, device(db, dm)).start())
        for dm in inc_peers:
            inc_copy(dm, chunk, m, device(0, dm)).start()

    def adjoint_cols(chunk):
        for db, dm in peers:
            owner = lax.rem(m - dm + mem_size, mem_size)
            when(-db, lambda db=db, dm=dm, owner=owner: weight_copy(
                db, dm, chunk, owner, device(-db, -dm)).wait_recv())
        span = rows_of(chunk)

        final = chunk == CHUNKS - 1

        def member(k, carry):
            fields = (halo[0, k, span, :], own_pert[k, span, :], halo[1, k, span, :])
            for block, field in enumerate(fields):
                product = field * weighted[block, span, :]
                adjoints[chunk][k, block * steps[chunk]:(block + 1) * steps[chunk], :] = dot(
                    product, col_table[...]
                ).astype(jnp.bfloat16)
            sums = dot(tables[chunk][...], adjoints[chunk][k])
            if chunk:
                sums += accumulated[k]
            if final:
                result[k] = sums.astype(jnp.bfloat16)
                out_copy(k).start()
            else:
                accumulated[k] = sums
            return carry

        lax.fori_loop(0, members, member, 0, unroll=UNROLL)

    def out_copy(k):
        return pltpu.make_async_copy(result.at[k], gradient.at[k], out_sem.at[k])

    for turn in range(CHUNKS + 2):
        if turn < CHUNKS:
            send_terms(turn, 2 * odd - 1, odd)
        if 0 <= turn - 1 < CHUNKS:
            send_weighted(turn - 1)
        if 0 <= turn - 2 < CHUNKS:
            adjoint_cols(turn - 2)

    for chunk in range(CHUNKS):
        for dm in inc_peers:
            owner = lax.rem(m - dm + mem_size, mem_size)
            inc_copy(dm, chunk, owner, device(0, -dm)).wait_recv()
    if increment.shape[1] == cols:
        view = total
    else:
        view = total.at[:, pl.ds(pl.multiple_of(m * share, share), share)]
    inc_out = pltpu.make_async_copy(view, increment, load_sem.at[0])
    inc_out.start()

    for chunk in range(CHUNKS):
        for db in (1, -1):
            when(db, lambda db=db, chunk=chunk: halo_copy(db, chunk, device(db, 0)).wait_send())
        for db, dm in peers:
            def sent(db=db, dm=dm, chunk=chunk):
                term_copy(db, dm, chunk, device(db, dm)).wait_send()
                weight_copy(db, dm, chunk, m, device(db, dm)).wait_send()
            when(db, sent)
        for dm in inc_peers:
            inc_copy(dm, chunk, m, device(0, dm)).wait_send()
    for k in range(members):
        out_copy(k).wait()
    inc_out.wait()


def deliver(gradient, increment, gradient_out, increment_out, held, held_increment, in_sem, out_sem):
    members = gradient.shape[0]
    steps = [(gradient.at[k], held.at[k], gradient_out.at[k]) for k in range(members)]
    steps.append((increment, held_increment, increment_out))
    arrivals = [pltpu.make_async_copy(src, mid, in_sem.at[n]) for n, (src, mid, _) in enumerate(steps)]
    leaves = [pltpu.make_async_copy(mid, dst, out_sem.at[n]) for n, (_, mid, dst) in enumerate(steps)]
    for copy in arrivals:
        copy.start()
    for arrival, leave in zip(arrivals, leaves):
        arrival.wait()
        leave.start()
    for leave in leaves:
        leave.wait()


def on_device(control, perturbations, innovation, error_weight):
    members, rows, cols = control.shape
    space_size = lax.axis_size("space")
    mem_size = lax.axis_size("mem")
    share = cols // mem_size
    aligned = share % 128 == 0
    steps = [rows * size // 8 for size in SIZES]
    slots = 3 * mem_size
    bf16, f32 = jnp.bfloat16, jnp.float32
    dma = pltpu.SemaphoreType.DMA
    gradient, increment = pl.pallas_call(
        functools.partial(kernel, space_size, mem_size, share),
        out_shape=(
            jax.ShapeDtypeStruct((members, rows, cols), bf16),
            jax.ShapeDtypeStruct((rows, share if aligned else cols), f32),
        ),
        in_specs=[pl.BlockSpec(memory_space=pltpu.HBM)] * 4,
        out_specs=(pl.BlockSpec(memory_space=pl.ANY),) * 2,
        scratch_shapes=[
            pltpu.VMEM((members, rows, cols), bf16),
            pltpu.VMEM((members, rows, cols), bf16),
            pltpu.VMEM((rows, cols), f32),
            pltpu.VMEM((rows, cols), f32),
            pltpu.VMEM((2, members, rows, cols), bf16),
            pltpu.VMEM((2, members, rows, cols), f32),
            pltpu.VMEM((rows, cols), f32),
            pltpu.VMEM((3, rows, cols), bf16),
            pltpu.VMEM((slots, rows, share) if aligned else (slots, rows // mem_size, cols), bf16),
            pltpu.VMEM((3, rows, cols), bf16),
            pltpu.VMEM((rows, cols), f32),
            pltpu.VMEM((members, rows, cols), bf16),
            pltpu.VMEM((cols, cols), bf16),
            pltpu.VMEM((rows, 3 * rows), bf16),
            *[pltpu.VMEM((rows, 3 * step), bf16) for step in steps],
            *[pltpu.VMEM((members, 3 * step, cols), bf16) for step in steps],
            pltpu.VMEM((members, rows, cols), f32),
            dma((4,)),
            dma((2, CHUNKS)),
            dma((2, CHUNKS)),
            dma((CHUNKS, slots)),
            dma((CHUNKS, slots)),
            dma((CHUNKS, slots)),
            dma((CHUNKS, slots)),
            dma((CHUNKS, mem_size)),
            dma((CHUNKS, mem_size)),
            dma((members,)),
        ],
        compiler_params=pltpu.CompilerParams(
            collective_id=0, has_side_effects=True, vmem_limit_bytes=60 * 1024 * 1024
        ),
    )(control, perturbations, innovation, error_weight)
    if not aligned:
        increment = lax.dynamic_slice_in_dim(increment, lax.axis_index("mem") * share, share, 1)
    return pl.pallas_call(
        deliver,
        out_shape=(
            jax.ShapeDtypeStruct((members, rows, cols), bf16),
            jax.ShapeDtypeStruct((rows, share), f32),
        ),
        in_specs=[pl.BlockSpec(memory_space=pl.ANY)] * 2,
        out_specs=(pl.BlockSpec(memory_space=pl.ANY),) * 2,
        scratch_shapes=[
            pltpu.VMEM((members, rows, cols), bf16),
            pltpu.VMEM((rows, share), f32),
            dma((members + 1,)),
            dma((members + 1,)),
        ],
    )(gradient, increment)


def solution(mesh):
    placed = (P("mem", "space", None), P("mem", "space", None), P("space", None), P("space", None))
    return jax.shard_map(
        on_device,
        mesh=mesh,
        in_specs=placed,
        out_specs=(P("mem", "space", None), P("space", "mem")),
        check_vma=False,
    )
```
